256 devices in a mesh: px: 16 (over y, z_hi), py: 16 (over x, z_lo, core).
Axes of the slice: x: 4, y: 4, z: 8 (z_hi: 4, z_lo: 2; z = z_hi * 2 + z_lo), core: 2. Of those that a mesh axis runs over, the one named last changes fastest.
Arguments:
- slab_start: int32 [1], replicated, may hold values from 0 to 96
- fixed_mask: int32 [128, 128, 128], P('px', 'py'), may hold values 0 or 1
- background: float32 [2, 128, 128, 128], P(None, 'px', 'py'), may hold values from -6 to 6
- observed: float32 [2, 128, 128, 128], P(None, 'px', 'py'), may hold values from -6 to 6
- kernel: float32 [2, 2, 256, 256, 256], P(None, None, 'px', 'py'), may hold values from -12 to 12
- frequencies: float32 [3, 128], replicated, may hold values from -48 to 48
- first_weight: bfloat16 [256, 256], replicated, may hold values from -0.375 to 0.375
- second_weight: bfloat16 [256, 256], replicated, may hold values from -0.375 to 0.375
- output_weight: bfloat16 [256, 2], replicated, may hold values from -0.375 to 0.375
Outputs:
- predicted: float32 [2, 128, 128, 128], P(None, 'px', 'py')
- grad_first: float32 [256, 256], replicated
- grad_second: float32 [256, 256], replicated
- grad_output: float32 [256, 2], replicated
The draws below stay inside these ranges and needn't reach their ends.
Inputs may be any that keep to these rules, and one draw needn't show every extreme that they name: `fixed_mask`: 1 where a cell outside the slab keeps its background value, 0 where it is empty.
All inputs are finite; a program needn't handle non-finite values. No bound on the sum of `fixed_mask` on one device may be relied on, other than what follows from the above.
Results may differ from the reference program's by a relative error of at most 0.0015.
Values sent between devices are 32-bit elements; how exact they have to be, the bound alone decides.
A program may use at most 64 MiB of HBM per device.

```python
import math
import jax
import jax.numpy as jnp
from jax import lax

M = 256
N = 128
SLAB = 32
FREQ = 128
FEAT = 256
HID = 256


def place_ends(drawn, own_key, low, top_value):
    shape = drawn.shape
    place = [jax.random.randint(jax.random.fold_in(own_key, axis), (), 0, shape[axis]) for axis in range(len(shape))]
    drawn = drawn.at[tuple(place)].set(low)
    longest = shape.index(max(shape))
    place[longest] = (place[longest] + 1) % shape[longest]
    return drawn.at[tuple(place)].set(top_value)


def block_scale(rng, dims, cuts, smallest, largest):
    level = 1.0
    for dim, parts in cuts:
        heights = jax.random.uniform(jax.random.fold_in(jax.random.fold_in(rng, 6), dim), (parts,), jnp.float32, smallest / len(cuts), largest / len(cuts))
        level = level * jnp.repeat(jnp.exp(heights), dims[dim] // parts).reshape((-1,) + (1,) * (len(dims) - 1 - dim))
    return level


def noise(stream_key, dims, deviation, limit, cuts=(), kind=jnp.bfloat16):
    loudness = block_scale(stream_key, dims, cuts, -0.22, 0.18) if cuts else 1.0
    drawn = jax.random.normal(stream_key, dims, jnp.float32) * deviation * loudness
    return jnp.minimum(jnp.maximum(drawn, -limit), limit).astype(kind)


def setup_inputs(seed: int = 0) -> dict:
    key_of = jax.random.split(jax.random.key(seed), 10)
    return {
        "slab_start": jax.random.randint(key_of[0], (1,), 0, N - SLAB + 1).astype(jnp.int32),
        "fixed_mask": place_ends((jax.random.randint(key_of[1], (N, N, N), 0, 4) < 3).astype(jnp.int32), jax.random.fold_in(key_of[1], 1), 0, 1),
        "background": noise(key_of[2], (2, N, N, N), 1.0, 6.0, ((1, 16), (2, 16)), jnp.float32),
        "observed": noise(key_of[3], (2, N, N, N), 1.0, 6.0, ((1, 16), (2, 16)), jnp.float32),
        "kernel": noise(key_of[4], (2, 2, M, M, M), 2.0, 12.0, ((2, 16), (3, 16)), jnp.float32),
        "frequencies": noise(key_of[5], (3, FREQ), 12.0, 48.0, (), jnp.float32),
        "first_weight": noise(key_of[6], (FEAT, HID), FEAT ** -0.5, 0.375),
        "second_weight": noise(key_of[7], (HID, HID), HID ** -0.5, 0.375),
        "output_weight": noise(key_of[8], (HID, 2), HID ** -0.5, 0.375),
    }


TWO_PI = 2.0 * math.pi


def apply_operator(fields, kernel, conjugate):
    outputs = []
    for field_index in range(2):
        padded = jnp.pad(fields[field_index], ((0, M - N), (0, M - N), (0, M - N)))
        spectrum = jnp.fft.fftn(padded)
        kernel_real = jnp.transpose(kernel[field_index, 0], (1, 2, 0))
        kernel_imag = jnp.transpose(kernel[field_index, 1], (1, 2, 0)) * conjugate
        product = spectrum * (kernel_real + 1j * kernel_imag)
        back = jnp.fft.ifftn(product).real[:N, :N, :N]
        outputs.append(back)
    return jnp.stack(outputs)


def plane_layers(x_value, frequencies, first_weight, second_weight):
    coord = jnp.arange(N, dtype=jnp.int32).astype(jnp.float32) / N
    phase = (x_value * frequencies[0] + coord[:, None, None] * frequencies[1] + coord[None, :, None] * frequencies[2]) * TWO_PI
    features = jnp.concatenate([jnp.sin(phase), jnp.cos(phase)], -1).astype(jnp.bfloat16).reshape(N * N, FEAT)
    hidden_one = jnp.tanh(jnp.dot(features, first_weight, preferred_element_type=jnp.float32)).astype(jnp.bfloat16)
    hidden_two = jnp.tanh(jnp.dot(hidden_one, second_weight, preferred_element_type=jnp.float32)).astype(jnp.bfloat16)
    return features, hidden_one, hidden_two


def reference(slab_start, fixed_mask, background, observed, kernel, frequencies, first_weight, second_weight, output_weight):
    first_plane = slab_start[0].astype(jnp.int32)
    planes = jnp.arange(SLAB, dtype=jnp.int32)

    def x_of(plane):
        return (first_plane + plane).astype(jnp.float32) / N

    def forward_plane(plane):
        features, hidden_one, hidden_two = plane_layers(x_of(plane), frequencies, first_weight, second_weight)
        return jnp.dot(hidden_two, output_weight, preferred_element_type=jnp.float32)

    network = lax.map(forward_plane, planes)
    slab_values = jnp.transpose(network.reshape(SLAB, N, N, 2), (3, 1, 2, 0))
    zero = jnp.zeros((), jnp.int32)
    base = fixed_mask.astype(jnp.float32) * background
    fields = lax.dynamic_update_slice(base, slab_values, (zero, zero, zero, first_plane))
    predicted = apply_operator(fields, kernel, 1.0)
    residual = (predicted - observed) / N
    adjoint = apply_operator(residual, kernel, -1.0)
    adjoint_slab = lax.dynamic_slice(adjoint, (zero, zero, zero, first_plane), (2, N, N, SLAB))
    adjoint_planes = jnp.transpose(adjoint_slab, (3, 0, 1, 2))

    def backward_plane(carry, inputs):
        plane, adjoint_plane = inputs
        features, hidden_one, hidden_two = plane_layers(x_of(plane), frequencies, first_weight, second_weight)
        cotangent = adjoint_plane.reshape(2, N * N).T.astype(jnp.bfloat16)
        grad_out = jnp.dot(hidden_two.T, cotangent, preferred_element_type=jnp.float32)
        back_two = jnp.dot(cotangent, output_weight.T, preferred_element_type=jnp.float32)
        two_values = hidden_two.astype(jnp.float32)
        delta_two = (back_two * (1.0 - two_values * two_values)).astype(jnp.bfloat16)
        grad_two = jnp.dot(hidden_one.T, delta_two, preferred_element_type=jnp.float32)
        back_one = jnp.dot(delta_two, second_weight.T, preferred_element_type=jnp.float32)
        one_values = hidden_one.astype(jnp.float32)
        delta_one = (back_one * (1.0 - one_values * one_values)).astype(jnp.bfloat16)
        grad_one = jnp.dot(features.T, delta_one, preferred_element_type=jnp.float32)
        return (carry[0] + grad_one, carry[1] + grad_two, carry[2] + grad_out), None

    start_carry = (jnp.zeros((FEAT, HID), jnp.float32), jnp.zeros((HID, HID), jnp.float32), jnp.zeros((HID, 2), jnp.float32))
    grads, unused = lax.scan(backward_plane, start_carry, (planes, adjoint_planes))
    return predicted, grads[0], grads[1], grads[2]
```

```python
import jax
import jax.numpy as jnp
from jax import lax
from jax.sharding import PartitionSpec as P

SLAB = 32
FEAT = 256
TWO_PI = 6.283185307179586
PRECISION = lax.Precision.HIGH


def angles(count_in, count_out, length):
    rows = lax.broadcasted_iota(jnp.int32, (count_in, count_out), 0)
    columns = lax.broadcasted_iota(jnp.int32, (count_in, count_out), 1)
    angle = (rows * columns % length).astype(jnp.float32) * (TWO_PI / length)
    return jnp.cos(angle), jnp.sin(angle)


def complex_table(count_in, count_out, length, sign):
    cosine, sine = angles(count_in, count_out, length)
    top = jnp.stack([cosine, sign * sine], 1)
    bottom = jnp.stack([-sign * sine, cosine], 1)
    return jnp.stack([top, bottom], 0)


def contract(form, values, table):
    return jnp.einsum(form, values, table, precision=PRECISION)


def round_trip(fields, kernel_real, kernel_imag, direction, tables, ranks):
    x_forward, y_forward, z_forward, z_inverse, y_inverse, x_inverse = tables
    px_size, py_size = ranks
    spectrum = contract("fyzx,xckl->kcfyzl", fields, x_forward)
    spectrum = lax.all_to_all(spectrum, "px", 0, 0, tiled=True)
    spectrum = contract("scfyzl,csydmq->mdfzlq", spectrum, y_forward)
    spectrum = lax.all_to_all(spectrum, "py", 0, 0, tiled=True)
    spectrum = contract("sdfzlq,dszek->eflqk", spectrum, z_forward)
    real_part = spectrum[0]
    imag_part = spectrum[1]
    product_real = kernel_real * real_part - direction * (kernel_imag * imag_part)
    product_imag = kernel_real * imag_part + direction * (kernel_imag * real_part)
    product = jnp.stack([product_real, product_imag], 0)
    back = contract("eflqk,ekgmz->mgflqz", product, z_inverse)
    back = lax.all_to_all(back, "py", 0, 0, tiled=True)
    back = contract("sgflqz,gsqhmy->mhfyzl", back, y_inverse)
    back = lax.all_to_all(back, "px", 0, 0, tiled=True)
    return contract("shfyzl,hslx->fyzx", back, x_inverse)


def gradient_sum(parts):
    flat = jnp.concatenate([part.reshape(-1) for part in parts])
    count = flat.shape[0]
    devices = lax.axis_size("px") * lax.axis_size("py")
    padded = jnp.pad(flat, (0, (-count) % devices))
    share = padded.shape[0] // devices
    summed = lax.all_to_all(padded.reshape(devices, share), ("px", "py"), 0, 0, tiled=True)
    summed = summed.sum(0)
    gathered = jnp.broadcast_to(summed[None], (devices, share))
    gathered = lax.all_to_all(gathered, ("px", "py"), 0, 0, tiled=True).reshape(-1)
    result = []
    offset = 0
    for part in parts:
        result.append(gathered[offset : offset + part.size].reshape(part.shape))
        offset += part.size
    return tuple(result)


def on_device(
    slab_start,
    fixed_mask,
    background,
    observed,
    kernel,
    frequencies,
    first_weight,
    second_weight,
    output_weight,
):
    y_count, z_count, grid = fixed_mask.shape
    length = kernel.shape[4]
    px_size = lax.axis_size("px")
    py_size = lax.axis_size("py")
    kx_count = kernel.shape[2]
    ky_count = kernel.shape[3]
    first_plane = slab_start[0]
    y_coord = (lax.axis_index("px") * y_count + jnp.arange(y_count, dtype=jnp.int32)).astype(
        jnp.float32
    ) / grid
    z_coord = (lax.axis_index("py") * z_count + jnp.arange(z_count, dtype=jnp.int32)).astype(
        jnp.float32
    ) / grid
    x_coord = (first_plane + jnp.arange(SLAB, dtype=jnp.int32)).astype(jnp.float32) / grid
    phase = (
        x_coord[None, None, :, None] * frequencies[0]
        + y_coord[:, None, None, None] * frequencies[1]
        + z_coord[None, :, None, None] * frequencies[2]
    ) * TWO_PI
    features = (
        jnp.concatenate([jnp.sin(phase), jnp.cos(phase)], -1).astype(jnp.bfloat16).reshape(-1, FEAT)
    )
    hidden_one = jnp.tanh(
        jnp.dot(features, first_weight, preferred_element_type=jnp.float32)
    ).astype(jnp.bfloat16)
    hidden_two = jnp.tanh(
        jnp.dot(hidden_one, second_weight, preferred_element_type=jnp.float32)
    ).astype(jnp.bfloat16)
    network = jnp.einsum("rh,hc->cr", hidden_two, output_weight, preferred_element_type=jnp.float32)
    slab_values = network.reshape(2, y_count, z_count, SLAB)
    zero = jnp.zeros((), jnp.int32)
    placed = lax.dynamic_update_slice(
        jnp.zeros((2, y_count, z_count, grid), jnp.float32),
        slab_values,
        (zero, zero, zero, first_plane),
    )
    plane_index = jnp.arange(grid, dtype=jnp.int32)
    inside = (plane_index >= first_plane) & (plane_index < first_plane + SLAB)
    fields = jnp.where(inside, placed, fixed_mask.astype(jnp.float32) * background)

    cosine, sine = angles(grid, length, length)
    x_forward = jnp.stack([cosine, -sine], 1).reshape(grid, 2, px_size, kx_count)
    y_forward = complex_table(grid, length, length, -1.0).reshape(
        2, px_size, y_count, 2, py_size, ky_count
    )
    z_forward = complex_table(grid, length, length, -1.0).reshape(2, py_size, z_count, 2, length)
    z_inverse = complex_table(length, grid, length, 1.0).reshape(2, length, 2, py_size, z_count)
    y_inverse = complex_table(length, grid, length, 1.0).reshape(
        2, py_size, ky_count, 2, px_size, y_count
    )
    x_inverse = (
        jnp.stack([cosine.T, -sine.T], 0) * (1.0 / float(length) ** 3)
    ).reshape(2, px_size, kx_count, grid)
    tables = (x_forward, y_forward, z_forward, z_inverse, y_inverse, x_inverse)
    ranks = (px_size, py_size)

    kernel_real = kernel[:, 0]
    kernel_imag = kernel[:, 1]
    predicted = round_trip(fields, kernel_real, kernel_imag, 1.0, tables, ranks)
    residual = (predicted - observed) / grid
    adjoint = round_trip(residual, kernel_real, kernel_imag, -1.0, tables, ranks)
    cotangent = (
        lax.dynamic_slice(adjoint, (zero, zero, zero, first_plane), (2, y_count, z_count, SLAB))
        .reshape(2, -1)
        .astype(jnp.bfloat16)
    )
    grad_output = jnp.einsum("rh,cr->hc", hidden_two, cotangent, preferred_element_type=jnp.float32)
    back_two = jnp.einsum("cr,hc->rh", cotangent, output_weight, preferred_element_type=jnp.float32)
    two_values = hidden_two.astype(jnp.float32)
    delta_two = (back_two * (1.0 - two_values * two_values)).astype(jnp.bfloat16)
    grad_second = jnp.einsum("rh,rk->hk", hidden_one, delta_two, preferred_element_type=jnp.float32)
    back_one = jnp.einsum("rk,hk->rh", delta_two, second_weight, preferred_element_type=jnp.float32)
    one_values = hidden_one.astype(jnp.float32)
    delta_one = (back_one * (1.0 - one_values * one_values)).astype(jnp.bfloat16)
    grad_first = jnp.einsum("rf,rh->fh", features, delta_one, preferred_element_type=jnp.float32)
    grad_first, grad_second, grad_output = gradient_sum((grad_first, grad_second, grad_output))
    return (predicted, grad_first, grad_second, grad_output)


def solution(mesh):
    return jax.shard_map(
        on_device,
        mesh=mesh,
        in_specs=(
            P(),
            P("px", "py", None),
            P(None, "px", "py", None),
            P(None, "px", "py", None),
            P(None, None, "px", "py", None),
            P(),
            P(),
            P(),
            P(),
        ),
        out_specs=(P(None, "px", "py", None), P(), P(), P()),
        check_vma=False,
    )
```

```python
import jax
import jax.numpy as jnp
from jax import lax
from jax.sharding import PartitionSpec as P

SLAB = 32
FEAT = 256
TWO_PI = 6.283185307179586
PRECISION = lax.Precision.HIGH


def angles(count_in, count_out, length):
    rows = lax.broadcasted_iota(jnp.int32, (count_in, count_out), 0)
    columns = lax.broadcasted_iota(jnp.int32, (count_in, count_out), 1)
    angle = (rows * columns % length).astype(jnp.float32) * (TWO_PI / length)
    return jnp.cos(angle), jnp.sin(angle)


def complex_table(count_in, count_out, length, sign):
    cosine, sine = angles(count_in, count_out, length)
    top = jnp.stack([cosine, sign * sine], 1)
    bottom = jnp.stack([-sign * sine, cosine], 1)
    return jnp.stack([top, bottom], 0)


def contract(form, values, table):
    return jnp.einsum(form, values, table, precision=PRECISION)


def round_trip(fields, kernel_real, kernel_imag, direction, tables, ranks):
    x_forward, y_forward, z_forward, z_inverse, y_inverse, x_inverse = tables
    px_size, py_size = ranks
    spectrum = contract("fyzx,xckl->kcfyzl", fields, x_forward)
    spectrum = lax.all_to_all(spectrum, "px", 0, 0, tiled=True)
    spectrum = contract("scfyzl,csydmq->mdfzlq", spectrum, y_forward)
    spectrum = lax.all_to_all(spectrum, "py", 0, 0, tiled=True)
    spectrum = contract("sdfzlq,dszek->eflqk", spectrum, z_forward)
    real_part = spectrum[0]
    imag_part = spectrum[1]
    product_real = kernel_real * real_part - direction * (kernel_imag * imag_part)
    product_imag = kernel_real * imag_part + direction * (kernel_imag * real_part)
    product = jnp.stack([product_real, product_imag], 0)
    back = contract("eflqk,ekgmz->mgflqz", product, z_inverse)
    back = lax.all_to_all(back, "py", 0, 0, tiled=True)
    back = contract("sgflqz,gsqhmy->mhfyzl", back, y_inverse)
    back = lax.all_to_all(back, "px", 0, 0, tiled=True)
    return contract("shfyzl,hslx->fyzx", back, x_inverse)


def gradient_sum(parts):
    devices = lax.axis_size("px") * lax.axis_size("py")
    joined = jnp.concatenate(parts, 1)
    rows, columns = joined.shape
    share = rows // devices
    summed = lax.all_to_all(joined.reshape(devices, share, columns), ("px", "py"), 0, 0, tiled=True)
    summed = summed.sum(0)
    gathered = jnp.broadcast_to(summed[None], (devices, share, columns))
    gathered = lax.all_to_all(gathered, ("px", "py"), 0, 0, tiled=True).reshape(rows, columns)
    result = []
    offset = 0
    for part in parts:
        result.append(gathered[:, offset : offset + part.shape[1]])
        offset += part.shape[1]
    return tuple(result)


def on_device(
    slab_start,
    fixed_mask,
    background,
    observed,
    kernel,
    frequencies,
    first_weight,
    second_weight,
    output_weight,
):
    y_count, z_count, grid = fixed_mask.shape
    length = kernel.shape[4]
    px_size = lax.axis_size("px")
    py_size = lax.axis_size("py")
    kx_count = kernel.shape[2]
    ky_count = kernel.shape[3]
    first_plane = slab_start[0]
    y_coord = (lax.axis_index("px") * y_count + jnp.arange(y_count, dtype=jnp.int32)).astype(
        jnp.float32
    ) / grid
    z_coord = (lax.axis_index("py") * z_count + jnp.arange(z_count, dtype=jnp.int32)).astype(
        jnp.float32
    ) / grid
    x_coord = (first_plane + jnp.arange(SLAB, dtype=jnp.int32)).astype(jnp.float32) / grid
    phase = (
        x_coord[None, None, :, None] * frequencies[0]
        + y_coord[:, None, None, None] * frequencies[1]
        + z_coord[None, :, None, None] * frequencies[2]
    ) * TWO_PI
    features = (
        jnp.concatenate([jnp.sin(phase), jnp.cos(phase)], -1).astype(jnp.bfloat16).reshape(-1, FEAT)
    )
    hidden_one = jnp.tanh(
        jnp.dot(features, first_weight, preferred_element_type=jnp.float32)
    ).astype(jnp.bfloat16)
    hidden_two = jnp.tanh(
        jnp.dot(hidden_one, second_weight, preferred_element_type=jnp.float32)
    ).astype(jnp.bfloat16)
    network = jnp.einsum("rh,hc->cr", hidden_two, output_weight, preferred_element_type=jnp.float32)
    slab_values = network.reshape(2, y_count, z_count, SLAB)
    zero = jnp.zeros((), jnp.int32)
    placed = lax.dynamic_update_slice(
        jnp.zeros((2, y_count, z_count, grid), jnp.float32),
        slab_values,
        (zero, zero, zero, first_plane),
    )
    plane_index = jnp.arange(grid, dtype=jnp.int32)
    inside = (plane_index >= first_plane) & (plane_index < first_plane + SLAB)
    fields = jnp.where(inside, placed, fixed_mask.astype(jnp.float32) * background)

    cosine, sine = angles(grid, length, length)
    x_forward = jnp.stack([cosine, -sine], 1).reshape(grid, 2, px_size, kx_count)
    y_forward = complex_table(grid, length, length, -1.0).reshape(
        2, px_size, y_count, 2, py_size, ky_count
    )
    z_forward = complex_table(grid, length, length, -1.0).reshape(2, py_size, z_count, 2, length)
    z_inverse = complex_table(length, grid, length, 1.0).reshape(2, length, 2, py_size, z_count)
    y_inverse = complex_table(length, grid, length, 1.0).reshape(
        2, py_size, ky_count, 2, px_size, y_count
    )
    x_inverse = (
        jnp.stack([cosine.T, -sine.T], 0) * (1.0 / float(length) ** 3)
    ).reshape(2, px_size, kx_count, grid)
    tables = (x_forward, y_forward, z_forward, z_inverse, y_inverse, x_inverse)
    ranks = (px_size, py_size)

    kernel_real = kernel[:, 0]
    kernel_imag = kernel[:, 1]
    predicted = round_trip(fields, kernel_real, kernel_imag, 1.0, tables, ranks)
    residual = (predicted - observed) / grid
    adjoint = round_trip(residual, kernel_real, kernel_imag, -1.0, tables, ranks)
    cotangent = (
        lax.dynamic_slice(adjoint, (zero, zero, zero, first_plane), (2, y_count, z_count, SLAB))
        .reshape(2, -1)
        .astype(jnp.bfloat16)
    )
    grad_output = jnp.einsum("rh,cr->hc", hidden_two, cotangent, preferred_element_type=jnp.float32)
    back_two = jnp.einsum("cr,hc->rh", cotangent, output_weight, preferred_element_type=jnp.float32)
    two_values = hidden_two.astype(jnp.float32)
    delta_two = (back_two * (1.0 - two_values * two_values)).astype(jnp.bfloat16)
    grad_second = jnp.einsum("rh,rk->hk", hidden_one, delta_two, preferred_element_type=jnp.float32)
    back_one = jnp.einsum("rk,hk->rh", delta_two, second_weight, preferred_element_type=jnp.float32)
    one_values = hidden_one.astype(jnp.float32)
    delta_one = (back_one * (1.0 - one_values * one_values)).astype(jnp.bfloat16)
    grad_first = jnp.einsum("rf,rh->fh", features, delta_one, preferred_element_type=jnp.float32)
    grad_first, grad_second, grad_output = gradient_sum((grad_first, grad_second, grad_output))
    return (predicted, grad_first, grad_second, grad_output)


def solution(mesh):
    return jax.shard_map(
        on_device,
        mesh=mesh,
        in_specs=(
            P(),
            P("px", "py", None),
            P(None, "px", "py", None),
            P(None, "px", "py", None),
            P(None, None, "px", "py", None),
            P(),
            P(),
            P(),
            P(),
        ),
        out_specs=(P(None, "px", "py", None), P(), P(), P()),
        check_vma=False,
    )
```

```python
import jax
import jax.numpy as jnp
from jax import lax
from jax.sharding import PartitionSpec as P

SLAB = 32
FEAT = 256
TWO_PI = 6.283185307179586
PRECISION = lax.Precision.HIGH


def angles(count_in, count_out, length):
    rows = lax.broadcasted_iota(jnp.int32, (count_in, count_out), 0)
    columns = lax.broadcasted_iota(jnp.int32, (count_in, count_out), 1)
    angle = (rows * columns % length).astype(jnp.float32) * (TWO_PI / length)
    return jnp.cos(angle), jnp.sin(angle)


def complex_table(count_in, count_out, length, sign):
    cosine, sine = angles(count_in, count_out, length)
    top = jnp.stack([cosine, sign * sine], 1)
    bottom = jnp.stack([-sign * sine, cosine], 1)
    return jnp.stack([top, bottom], 0)


def contract(form, values, table):
    return jnp.einsum(form, values, table, precision=PRECISION)


def exchange(values, axis_name):
    shape = values.shape
    rows = values.reshape(shape[0], -1, 128)
    rows = lax.all_to_all(rows, axis_name, 0, 0, tiled=True)
    return rows.reshape(shape)


def round_trip(fields, kernel_real, kernel_imag, direction, tables, ranks):
    x_forward, y_forward, z_forward, z_inverse, y_inverse, x_inverse = tables
    px_size, py_size = ranks
    spectrum = contract("fyzx,xckl->kcfyzl", fields, x_forward)
    spectrum = exchange(spectrum, "px")
    spectrum = contract("scfyzl,csydmq->mdfzlq", spectrum, y_forward)
    spectrum = exchange(spectrum, "py")
    spectrum = contract("sdfzlq,dszek->eflqk", spectrum, z_forward)
    real_part = spectrum[0]
    imag_part = spectrum[1]
    product_real = kernel_real * real_part - direction * (kernel_imag * imag_part)
    product_imag = kernel_real * imag_part + direction * (kernel_imag * real_part)
    product = jnp.stack([product_real, product_imag], 0)
    back = contract("eflqk,ekgmz->mgflqz", product, z_inverse)
    back = exchange(back, "py")
    back = contract("sgflqz,gsqhmy->mhfyzl", back, y_inverse)
    back = exchange(back, "px")
    return contract("shfyzl,hslx->fyzx", back, x_inverse)


def gradient_sum(parts):
    devices = lax.axis_size("px") * lax.axis_size("py")
    joined = jnp.concatenate(parts, 1)
    rows, columns = joined.shape
    share = rows // devices
    summed = lax.all_to_all(joined.reshape(devices, share, columns), ("px", "py"), 0, 0, tiled=True)
    summed = summed.sum(0)
    gathered = jnp.broadcast_to(summed[None], (devices, share, columns))
    gathered = lax.all_to_all(gathered, ("px", "py"), 0, 0, tiled=True).reshape(rows, columns)
    result = []
    offset = 0
    for part in parts:
        result.append(gathered[:, offset : offset + part.shape[1]])
        offset += part.shape[1]
    return tuple(result)


def on_device(
    slab_start,
    fixed_mask,
    background,
    observed,
    kernel,
    frequencies,
    first_weight,
    second_weight,
    output_weight,
):
    y_count, z_count, grid = fixed_mask.shape
    length = kernel.shape[4]
    px_size = lax.axis_size("px")
    py_size = lax.axis_size("py")
    kx_count = kernel.shape[2]
    ky_count = kernel.shape[3]
    first_plane = slab_start[0]
    y_coord = (lax.axis_index("px") * y_count + jnp.arange(y_count, dtype=jnp.int32)).astype(
        jnp.float32
    ) / grid
    z_coord = (lax.axis_index("py") * z_count + jnp.arange(z_count, dtype=jnp.int32)).astype(
        jnp.float32
    ) / grid
    x_coord = (first_plane + jnp.arange(SLAB, dtype=jnp.int32)).astype(jnp.float32) / grid
    phase = (
        x_coord[None, None, :, None] * frequencies[0]
        + y_coord[:, None, None, None] * frequencies[1]
        + z_coord[None, :, None, None] * frequencies[2]
    ) * TWO_PI
    features = (
        jnp.concatenate([jnp.sin(phase), jnp.cos(phase)], -1).astype(jnp.bfloat16).reshape(-1, FEAT)
    )
    hidden_one = jnp.tanh(
        jnp.dot(features, first_weight, preferred_element_type=jnp.float32)
    ).astype(jnp.bfloat16)
    hidden_two = jnp.tanh(
        jnp.dot(hidden_one, second_weight, preferred_element_type=jnp.float32)
    ).astype(jnp.bfloat16)
    network = jnp.einsum("rh,hc->cr", hidden_two, output_weight, preferred_element_type=jnp.float32)
    slab_values = network.reshape(2, y_count, z_count, SLAB)
    zero = jnp.zeros((), jnp.int32)
    placed = lax.dynamic_update_slice(
        jnp.zeros((2, y_count, z_count, grid), jnp.float32),
        slab_values,
        (zero, zero, zero, first_plane),
    )
    plane_index = jnp.arange(grid, dtype=jnp.int32)
    inside = (plane_index >= first_plane) & (plane_index < first_plane + SLAB)
    fields = jnp.where(inside, placed, fixed_mask.astype(jnp.float32) * background)

    cosine, sine = angles(grid, length, length)
    x_forward = jnp.stack([cosine, -sine], 1).reshape(grid, 2, px_size, kx_count)
    y_forward = complex_table(grid, length, length, -1.0).reshape(
        2, px_size, y_count, 2, py_size, ky_count
    )
    z_forward = complex_table(grid, length, length, -1.0).reshape(2, py_size, z_count, 2, length)
    z_inverse = complex_table(length, grid, length, 1.0).reshape(2, length, 2, py_size, z_count)
    y_inverse = complex_table(length, grid, length, 1.0).reshape(
        2, py_size, ky_count, 2, px_size, y_count
    )
    x_inverse = (
        jnp.stack([cosine.T, -sine.T], 0) * (1.0 / float(length) ** 3)
    ).reshape(2, px_size, kx_count, grid)
    tables = (x_forward, y_forward, z_forward, z_inverse, y_inverse, x_inverse)
    ranks = (px_size, py_size)

    kernel_real = kernel[:, 0]
    kernel_imag = kernel[:, 1]
    predicted = round_trip(fields, kernel_real, kernel_imag, 1.0, tables, ranks)
    residual = (predicted - observed) / grid
    adjoint = round_trip(residual, kernel_real, kernel_imag, -1.0, tables, ranks)
    cotangent = (
        lax.dynamic_slice(adjoint, (zero, zero, zero, first_plane), (2, y_count, z_count, SLAB))
        .reshape(2, -1)
        .astype(jnp.bfloat16)
    )
    grad_output = jnp.einsum("rh,cr->hc", hidden_two, cotangent, preferred_element_type=jnp.float32)
    back_two = jnp.einsum("cr,hc->rh", cotangent, output_weight, preferred_element_type=jnp.float32)
    two_values = hidden_two.astype(jnp.float32)
    delta_two = (back_two * (1.0 - two_values * two_values)).astype(jnp.bfloat16)
    grad_second = jnp.einsum("rh,rk->hk", hidden_one, delta_two, preferred_element_type=jnp.float32)
    back_one = jnp.einsum("rk,hk->rh", delta_two, second_weight, preferred_element_type=jnp.float32)
    one_values = hidden_one.astype(jnp.float32)
    delta_one = (back_one * (1.0 - one_values * one_values)).astype(jnp.bfloat16)
    grad_first = jnp.einsum("rf,rh->fh", features, delta_one, preferred_element_type=jnp.float32)
    grad_first, grad_second, grad_output = gradient_sum((grad_first, grad_second, grad_output))
    return (predicted, grad_first, grad_second, grad_output)


def solution(mesh):
    return jax.shard_map(
        on_device,
        mesh=mesh,
        in_specs=(
            P(),
            P("px", "py", None),
            P(None, "px", "py", None),
            P(None, "px", "py", None),
            P(None, None, "px", "py", None),
            P(),
            P(),
            P(),
            P(),
        ),
        out_specs=(P(None, "px", "py", None), P(), P(), P()),
        check_vma=False,
    )
```

```python
import jax
import jax.numpy as jnp
from jax import lax
from jax.sharding import PartitionSpec as P

SLAB = 32
FEAT = 256
TWO_PI = 6.283185307179586
PRECISION = lax.Precision.HIGH


def angles(count_in, count_out, length):
    rows = lax.broadcasted_iota(jnp.int32, (count_in, count_out), 0)
    columns = lax.broadcasted_iota(jnp.int32, (count_in, count_out), 1)
    angle = (rows * columns % length).astype(jnp.float32) * (TWO_PI / length)
    return jnp.cos(angle), jnp.sin(angle)


def complex_table(count_in, count_out, length, sign):
    cosine, sine = angles(count_in, count_out, length)
    top = jnp.stack([cosine, sign * sine], 1)
    bottom = jnp.stack([-sign * sine, cosine], 1)
    return jnp.stack([top, bottom], 0)


def contract(form, values, table):
    return jnp.einsum(form, values, table, precision=PRECISION)


def round_trip(fields, kernel_real, kernel_imag, direction, tables, ranks):
    x_forward, y_forward, z_forward, z_inverse, y_inverse, x_inverse = tables
    px_size, py_size = ranks
    spectrum = contract("fyzx,xckl->kcyfzl", fields, x_forward)
    spectrum = lax.all_to_all(spectrum, "px", 0, 0, tiled=True)
    shape = spectrum.shape
    rows = shape[0] * shape[1] * shape[2]
    spectrum = jnp.dot(y_forward, spectrum.reshape(rows, -1), precision=PRECISION)
    spectrum = spectrum.reshape((py_size, 2, y_forward.shape[0] // (2 * py_size)) + shape[3:])
    spectrum = lax.all_to_all(spectrum, "py", 0, 0, tiled=True)
    spectrum = contract("sdqfzl,dszek->eflqk", spectrum, z_forward)
    real_part = spectrum[0]
    imag_part = spectrum[1]
    product_real = kernel_real * real_part - direction * (kernel_imag * imag_part)
    product_imag = kernel_real * imag_part + direction * (kernel_imag * real_part)
    product = jnp.stack([product_real, product_imag], 0)
    back = contract("eflqk,ekgmz->mgqflz", product, z_inverse)
    back = lax.all_to_all(back, "py", 0, 0, tiled=True)
    shape = back.shape
    rows = shape[0] * shape[1] * shape[2]
    back = jnp.dot(y_inverse, back.reshape(rows, -1), precision=PRECISION)
    back = back.reshape((px_size, 2, y_inverse.shape[0] // (2 * px_size)) + shape[3:])
    back = lax.all_to_all(back, "px", 0, 0, tiled=True)
    return contract("shyflz,hslx->fyzx", back, x_inverse)


def gradient_sum(parts):
    devices = lax.axis_size("px") * lax.axis_size("py")
    joined = jnp.concatenate(parts, 1)
    rows, columns = joined.shape
    share = rows // devices
    summed = lax.all_to_all(joined.reshape(devices, share, columns), ("px", "py"), 0, 0, tiled=True)
    summed = summed.sum(0)
    gathered = jnp.broadcast_to(summed[None], (devices, share, columns))
    gathered = lax.all_to_all(gathered, ("px", "py"), 0, 0, tiled=True).reshape(rows, columns)
    result = []
    offset = 0
    for part in parts:
        result.append(gathered[:, offset : offset + part.shape[1]])
        offset += part.shape[1]
    return tuple(result)


def on_device(
    slab_start,
    fixed_mask,
    background,
    observed,
    kernel,
    frequencies,
    first_weight,
    second_weight,
    output_weight,
):
    y_count, z_count, grid = fixed_mask.shape
    length = kernel.shape[4]
    px_size = lax.axis_size("px")
    py_size = lax.axis_size("py")
    kx_count = kernel.shape[2]
    ky_count = kernel.shape[3]
    first_plane = slab_start[0]
    y_coord = (lax.axis_index("px") * y_count + jnp.arange(y_count, dtype=jnp.int32)).astype(
        jnp.float32
    ) / grid
    z_coord = (lax.axis_index("py") * z_count + jnp.arange(z_count, dtype=jnp.int32)).astype(
        jnp.float32
    ) / grid
    x_coord = (first_plane + jnp.arange(SLAB, dtype=jnp.int32)).astype(jnp.float32) / grid
    phase = (
        x_coord[None, None, :, None] * frequencies[0]
        + y_coord[:, None, None, None] * frequencies[1]
        + z_coord[None, :, None, None] * frequencies[2]
    ) * TWO_PI
    features = (
        jnp.concatenate([jnp.sin(phase), jnp.cos(phase)], -1).astype(jnp.bfloat16).reshape(-1, FEAT)
    )
    hidden_one = jnp.tanh(
        jnp.dot(features, first_weight, preferred_element_type=jnp.float32)
    ).astype(jnp.bfloat16)
    hidden_two = jnp.tanh(
        jnp.dot(hidden_one, second_weight, preferred_element_type=jnp.float32)
    ).astype(jnp.bfloat16)
    network = jnp.einsum("rh,hc->cr", hidden_two, output_weight, preferred_element_type=jnp.float32)
    slab_values = network.reshape(2, y_count, z_count, SLAB)
    zero = jnp.zeros((), jnp.int32)
    placed = lax.dynamic_update_slice(
        jnp.zeros((2, y_count, z_count, grid), jnp.float32),
        slab_values,
        (zero, zero, zero, first_plane),
    )
    plane_index = jnp.arange(grid, dtype=jnp.int32)
    inside = (plane_index >= first_plane) & (plane_index < first_plane + SLAB)
    fields = jnp.where(inside, placed, fixed_mask.astype(jnp.float32) * background)

    cosine, sine = angles(grid, length, length)
    x_forward = jnp.stack([cosine, -sine], 1).reshape(grid, 2, px_size, kx_count)
    y_forward = complex_table(grid, length, length, -1.0).reshape(
        2, px_size, y_count, 2, py_size, ky_count
    )
    y_forward = jnp.transpose(y_forward, (4, 3, 5, 1, 0, 2)).reshape(2 * length, 2 * grid)
    z_forward = complex_table(grid, length, length, -1.0).reshape(2, py_size, z_count, 2, length)
    z_inverse = complex_table(length, grid, length, 1.0).reshape(2, length, 2, py_size, z_count)
    y_inverse = complex_table(length, grid, length, 1.0).reshape(
        2, py_size, ky_count, 2, px_size, y_count
    )
    y_inverse = jnp.transpose(y_inverse, (4, 3, 5, 1, 0, 2)).reshape(2 * grid, 2 * length)
    x_inverse = (
        jnp.stack([cosine.T, -sine.T], 0) * (1.0 / float(length) ** 3)
    ).reshape(2, px_size, kx_count, grid)
    tables = (x_forward, y_forward, z_forward, z_inverse, y_inverse, x_inverse)
    ranks = (px_size, py_size)

    kernel_real = kernel[:, 0]
    kernel_imag = kernel[:, 1]
    predicted = round_trip(fields, kernel_real, kernel_imag, 1.0, tables, ranks)
    residual = (predicted - observed) / grid
    adjoint = round_trip(residual, kernel_real, kernel_imag, -1.0, tables, ranks)
    cotangent = (
        lax.dynamic_slice(adjoint, (zero, zero, zero, first_plane), (2, y_count, z_count, SLAB))
        .reshape(2, -1)
        .astype(jnp.bfloat16)
    )
    grad_output = jnp.einsum("rh,cr->hc", hidden_two, cotangent, preferred_element_type=jnp.float32)
    back_two = jnp.einsum("cr,hc->rh", cotangent, output_weight, preferred_element_type=jnp.float32)
    two_values = hidden_two.astype(jnp.float32)
    delta_two = (back_two * (1.0 - two_values * two_values)).astype(jnp.bfloat16)
    grad_second = jnp.einsum("rh,rk->hk", hidden_one, delta_two, preferred_element_type=jnp.float32)
    back_one = jnp.einsum("rk,hk->rh", delta_two, second_weight, preferred_element_type=jnp.float32)
    one_values = hidden_one.astype(jnp.float32)
    delta_one = (back_one * (1.0 - one_values * one_values)).astype(jnp.bfloat16)
    grad_first = jnp.einsum("rf,rh->fh", features, delta_one, preferred_element_type=jnp.float32)
    grad_first, grad_second, grad_output = gradient_sum((grad_first, grad_second, grad_output))
    return (predicted, grad_first, grad_second, grad_output)


def solution(mesh):
    return jax.shard_map(
        on_device,
        mesh=mesh,
        in_specs=(
            P(),
            P("px", "py", None),
            P(None, "px", "py", None),
            P(None, "px", "py", None),
            P(None, None, "px", "py", None),
            P(),
            P(),
            P(),
            P(),
        ),
        out_specs=(P(None, "px", "py", None), P(), P(), P()),
        check_vma=False,
    )
```

```python
import jax
import jax.numpy as jnp
from jax import lax
from jax.sharding import PartitionSpec as P

SLAB = 32
FEAT = 256
TWO_PI = 6.283185307179586
PRECISION = lax.Precision.HIGH


def angles(count_in, count_out, length):
    rows = lax.broadcasted_iota(jnp.int32, (count_in, count_out), 0)
    columns = lax.broadcasted_iota(jnp.int32, (count_in, count_out), 1)
    angle = (rows * columns % length).astype(jnp.float32) * (TWO_PI / length)
    return jnp.cos(angle), jnp.sin(angle)


def complex_table(count_in, count_out, length, sign):
    cosine, sine = angles(count_in, count_out, length)
    top = jnp.stack([cosine, sign * sine], 1)
    bottom = jnp.stack([-sign * sine, cosine], 1)
    return jnp.stack([top, bottom], 0)


def contract(form, values, table):
    return jnp.einsum(form, values, table, precision=PRECISION)


def round_trip(fields, kernel_real, kernel_imag, direction, tables, ranks, x_inverse=None):
    x_forward, y_forward, z_forward, z_inverse, y_inverse, x_full = tables
    if x_inverse is None:
        x_inverse = x_full
    px_size, py_size = ranks
    spectrum = contract("fyzx,xckl->kcfyzl", fields, x_forward)
    spectrum = lax.all_to_all(spectrum, "px", 0, 0, tiled=True)
    spectrum = contract("scfyzl,csydmq->mdfzlq", spectrum, y_forward)
    spectrum = lax.all_to_all(spectrum, "py", 0, 0, tiled=True)
    spectrum = contract("sdfzlq,dszek->eflqk", spectrum, z_forward)
    real_part = spectrum[0]
    imag_part = spectrum[1]
    product_real = kernel_real * real_part - direction * (kernel_imag * imag_part)
    product_imag = kernel_real * imag_part + direction * (kernel_imag * real_part)
    product = jnp.stack([product_real, product_imag], 0)
    back = contract("eflqk,ekgmz->mgflqz", product, z_inverse)
    back = lax.all_to_all(back, "py", 0, 0, tiled=True)
    back = contract("sgflqz,gsqhmy->mhlfyz", back, y_inverse)
    back = lax.all_to_all(back, "px", 0, 0, tiled=True)
    return contract("shlfyz,hslx->fyzx", back, x_inverse)


def gradient_sum(parts):
    devices = lax.axis_size("px") * lax.axis_size("py")
    joined = jnp.concatenate(parts, 1)
    rows, columns = joined.shape
    share = rows // devices
    summed = lax.all_to_all(joined.reshape(devices, share, columns), ("px", "py"), 0, 0, tiled=True)
    summed = summed.sum(0)
    gathered = jnp.broadcast_to(summed[None], (devices, share, columns))
    gathered = lax.all_to_all(gathered, ("px", "py"), 0, 0, tiled=True).reshape(rows, columns)
    result = []
    offset = 0
    for part in parts:
        result.append(gathered[:, offset : offset + part.shape[1]])
        offset += part.shape[1]
    return tuple(result)


def on_device(
    slab_start,
    fixed_mask,
    background,
    observed,
    kernel,
    frequencies,
    first_weight,
    second_weight,
    output_weight,
):
    y_count, z_count, grid = fixed_mask.shape
    length = kernel.shape[4]
    px_size = lax.axis_size("px")
    py_size = lax.axis_size("py")
    kx_count = kernel.shape[2]
    ky_count = kernel.shape[3]
    first_plane = slab_start[0]
    y_coord = (lax.axis_index("px") * y_count + jnp.arange(y_count, dtype=jnp.int32)).astype(
        jnp.float32
    ) / grid
    z_coord = (lax.axis_index("py") * z_count + jnp.arange(z_count, dtype=jnp.int32)).astype(
        jnp.float32
    ) / grid
    x_coord = (first_plane + jnp.arange(SLAB, dtype=jnp.int32)).astype(jnp.float32) / grid
    phase = (
        x_coord[None, None, :, None] * frequencies[0]
        + y_coord[:, None, None, None] * frequencies[1]
        + z_coord[None, :, None, None] * frequencies[2]
    ) * TWO_PI
    features = (
        jnp.concatenate([jnp.sin(phase), jnp.cos(phase)], -1).astype(jnp.bfloat16).reshape(-1, FEAT)
    )
    hidden_one = jnp.tanh(
        jnp.dot(features, first_weight, preferred_element_type=jnp.float32)
    ).astype(jnp.bfloat16)
    hidden_two = jnp.tanh(
        jnp.dot(hidden_one, second_weight, preferred_element_type=jnp.float32)
    ).astype(jnp.bfloat16)
    network = jnp.einsum("rh,hc->cr", hidden_two, output_weight, preferred_element_type=jnp.float32)
    slab_values = network.reshape(2, y_count, z_count, SLAB)
    zero = jnp.zeros((), jnp.int32)
    placed = lax.dynamic_update_slice(
        jnp.zeros((2, y_count, z_count, grid), jnp.float32),
        slab_values,
        (zero, zero, zero, first_plane),
    )
    plane_index = jnp.arange(grid, dtype=jnp.int32)
    inside = (plane_index >= first_plane) & (plane_index < first_plane + SLAB)
    fields = jnp.where(inside, placed, fixed_mask.astype(jnp.float32) * background)

    cosine, sine = angles(grid, length, length)
    x_forward = jnp.stack([cosine, -sine], 1).reshape(grid, 2, px_size, kx_count)
    y_forward = complex_table(grid, length, length, -1.0).reshape(
        2, px_size, y_count, 2, py_size, ky_count
    )
    z_forward = complex_table(grid, length, length, -1.0).reshape(2, py_size, z_count, 2, length)
    z_inverse = complex_table(length, grid, length, 1.0).reshape(2, length, 2, py_size, z_count)
    y_inverse = complex_table(length, grid, length, 1.0).reshape(
        2, py_size, ky_count, 2, px_size, y_count
    )
    x_inverse = (
        jnp.stack([cosine.T, -sine.T], 0) * (1.0 / float(length) ** 3)
    ).reshape(2, px_size, kx_count, grid)
    tables = (x_forward, y_forward, z_forward, z_inverse, y_inverse, x_inverse)
    ranks = (px_size, py_size)

    kernel_real = kernel[:, 0]
    kernel_imag = kernel[:, 1]
    predicted = round_trip(fields, kernel_real, kernel_imag, 1.0, tables, ranks)
    residual = (predicted - observed) / grid
    slab_inverse = lax.dynamic_slice(x_inverse, (zero, zero, zero, first_plane), (2, px_size, kx_count, SLAB))
    adjoint_slab = round_trip(residual, kernel_real, kernel_imag, -1.0, tables, ranks, slab_inverse)
    cotangent = adjoint_slab.reshape(2, -1).astype(jnp.bfloat16)
    grad_output = jnp.einsum("rh,cr->hc", hidden_two, cotangent, preferred_element_type=jnp.float32)
    back_two = jnp.einsum("cr,hc->rh", cotangent, output_weight, preferred_element_type=jnp.float32)
    two_values = hidden_two.astype(jnp.float32)
    delta_two = (back_two * (1.0 - two_values * two_values)).astype(jnp.bfloat16)
    grad_second = jnp.einsum("rh,rk->hk", hidden_one, delta_two, preferred_element_type=jnp.float32)
    back_one = jnp.einsum("rk,hk->rh", delta_two, second_weight, preferred_element_type=jnp.float32)
    one_values = hidden_one.astype(jnp.float32)
    delta_one = (back_one * (1.0 - one_values * one_values)).astype(jnp.bfloat16)
    grad_first = jnp.einsum("rf,rh->fh", features, delta_one, preferred_element_type=jnp.float32)
    grad_first, grad_second, grad_output = gradient_sum((grad_first, grad_second, grad_output))
    return (predicted, grad_first, grad_second, grad_output)


def solution(mesh):
    return jax.shard_map(
        on_device,
        mesh=mesh,
        in_specs=(
            P(),
            P("px", "py", None),
            P(None, "px", "py", None),
            P(None, "px", "py", None),
            P(None, None, "px", "py", None),
            P(),
            P(),
            P(),
            P(),
        ),
        out_specs=(P(None, "px", "py", None), P(), P(), P()),
        check_vma=False,
    )
```

```python
import jax
import jax.numpy as jnp
from jax import lax
from jax.sharding import PartitionSpec as P

SLAB = 32
FEAT = 256
TWO_PI = 6.283185307179586
PRECISION = lax.Precision.HIGH


def angles(count_in, count_out, length):
    rows = lax.broadcasted_iota(jnp.int32, (count_in, count_out), 0)
    columns = lax.broadcasted_iota(jnp.int32, (count_in, count_out), 1)
    angle = (rows * columns % length).astype(jnp.float32) * (TWO_PI / length)
    return jnp.cos(angle), jnp.sin(angle)


def complex_table(count_in, count_out, length, sign):
    cosine, sine = angles(count_in, count_out, length)
    top = jnp.stack([cosine, sign * sine], 1)
    bottom = jnp.stack([-sign * sine, cosine], 1)
    return jnp.stack([top, bottom], 0)


def contract(form, values, table):
    return jnp.einsum(form, values, table, precision=PRECISION)


def exchange(values, axis_name):
    shape = values.shape
    rows = values.reshape(shape[0], -1, 128)
    rows = lax.all_to_all(rows, axis_name, 0, 0, tiled=True)
    return rows.reshape(shape)


def round_trip(fields, kernel_real, kernel_imag, direction, tables, ranks, x_inverse=None):
    x_forward, y_forward, z_forward, z_inverse, y_inverse, x_full = tables
    if x_inverse is None:
        x_inverse = x_full
    px_size, py_size = ranks
    spectrum = contract("fyzx,xckl->kcfyzl", fields, x_forward)
    spectrum = lax.all_to_all(spectrum, "px", 0, 0, tiled=True)
    spectrum = contract("scfyzl,csydmq->mdfzlq", spectrum, y_forward)
    spectrum = lax.all_to_all(spectrum, "py", 0, 0, tiled=True)
    spectrum = contract("sdfzlq,dszek->eflqk", spectrum, z_forward)
    real_part = spectrum[0]
    imag_part = spectrum[1]
    product_real = kernel_real * real_part - direction * (kernel_imag * imag_part)
    product_imag = kernel_real * imag_part + direction * (kernel_imag * real_part)
    product = jnp.stack([product_real, product_imag], 0)
    back = contract("eflqk,ekgmz->mgflqz", product, z_inverse)
    back = exchange(back, "py")
    back = contract("sgflqz,gsqhmy->mhlfyz", back, y_inverse)
    back = exchange(back, "px")
    return contract("shlfyz,hslx->fyzx", back, x_inverse)


def gradient_sum(parts):
    devices = lax.axis_size("px") * lax.axis_size("py")
    joined = jnp.concatenate(parts, 1)
    rows, columns = joined.shape
    share = rows // devices
    summed = lax.all_to_all(joined.reshape(devices, share, columns), ("px", "py"), 0, 0, tiled=True)
    summed = summed.sum(0)
    gathered = jnp.broadcast_to(summed[None], (devices, share, columns))
    gathered = lax.all_to_all(gathered, ("px", "py"), 0, 0, tiled=True).reshape(rows, columns)
    result = []
    offset = 0
    for part in parts:
        result.append(gathered[:, offset : offset + part.shape[1]])
        offset += part.shape[1]
    return tuple(result)


def on_device(
    slab_start,
    fixed_mask,
    background,
    observed,
    kernel,
    frequencies,
    first_weight,
    second_weight,
    output_weight,
):
    y_count, z_count, grid = fixed_mask.shape
    length = kernel.shape[4]
    px_size = lax.axis_size("px")
    py_size = lax.axis_size("py")
    kx_count = kernel.shape[2]
    ky_count = kernel.shape[3]
    first_plane = slab_start[0]
    y_coord = (lax.axis_index("px") * y_count + jnp.arange(y_count, dtype=jnp.int32)).astype(
        jnp.float32
    ) / grid
    z_coord = (lax.axis_index("py") * z_count + jnp.arange(z_count, dtype=jnp.int32)).astype(
        jnp.float32
    ) / grid
    x_coord = (first_plane + jnp.arange(SLAB, dtype=jnp.int32)).astype(jnp.float32) / grid
    phase = (
        x_coord[None, None, :, None] * frequencies[0]
        + y_coord[:, None, None, None] * frequencies[1]
        + z_coord[None, :, None, None] * frequencies[2]
    ) * TWO_PI
    features = (
        jnp.concatenate([jnp.sin(phase), jnp.cos(phase)], -1).astype(jnp.bfloat16).reshape(-1, FEAT)
    )
    hidden_one = jnp.tanh(
        jnp.dot(features, first_weight, preferred_element_type=jnp.float32)
    ).astype(jnp.bfloat16)
    hidden_two = jnp.tanh(
        jnp.dot(hidden_one, second_weight, preferred_element_type=jnp.float32)
    ).astype(jnp.bfloat16)
    network = jnp.einsum("rh,hc->cr", hidden_two, output_weight, preferred_element_type=jnp.float32)
    slab_values = network.reshape(2, y_count, z_count, SLAB)
    zero = jnp.zeros((), jnp.int32)
    placed = lax.dynamic_update_slice(
        jnp.zeros((2, y_count, z_count, grid), jnp.float32),
        slab_values,
        (zero, zero, zero, first_plane),
    )
    plane_index = jnp.arange(grid, dtype=jnp.int32)
    inside = (plane_index >= first_plane) & (plane_index < first_plane + SLAB)
    fields = jnp.where(inside, placed, fixed_mask.astype(jnp.float32) * background)

    cosine, sine = angles(grid, length, length)
    x_forward = jnp.stack([cosine, -sine], 1).reshape(grid, 2, px_size, kx_count)
    y_forward = complex_table(grid, length, length, -1.0).reshape(
        2, px_size, y_count, 2, py_size, ky_count
    )
    z_forward = complex_table(grid, length, length, -1.0).reshape(2, py_size, z_count, 2, length)
    z_inverse = complex_table(length, grid, length, 1.0).reshape(2, length, 2, py_size, z_count)
    y_inverse = complex_table(length, grid, length, 1.0).reshape(
        2, py_size, ky_count, 2, px_size, y_count
    )
    x_inverse = (
        jnp.stack([cosine.T, -sine.T], 0) * (1.0 / float(length) ** 3)
    ).reshape(2, px_size, kx_count, grid)
    tables = (x_forward, y_forward, z_forward, z_inverse, y_inverse, x_inverse)
    ranks = (px_size, py_size)

    kernel_real = kernel[:, 0]
    kernel_imag = kernel[:, 1]
    predicted = round_trip(fields, kernel_real, kernel_imag, 1.0, tables, ranks)
    residual = (predicted - observed) / grid
    slab_inverse = lax.dynamic_slice(x_inverse, (zero, zero, zero, first_plane), (2, px_size, kx_count, SLAB))
    adjoint_slab = round_trip(residual, kernel_real, kernel_imag, -1.0, tables, ranks, slab_inverse)
    cotangent = adjoint_slab.reshape(2, -1).astype(jnp.bfloat16)
    grad_output = jnp.einsum("rh,cr->hc", hidden_two, cotangent, preferred_element_type=jnp.float32)
    back_two = jnp.einsum("cr,hc->rh", cotangent, output_weight, preferred_element_type=jnp.float32)
    two_values = hidden_two.astype(jnp.float32)
    delta_two = (back_two * (1.0 - two_values * two_values)).astype(jnp.bfloat16)
    grad_second = jnp.einsum("rh,rk->hk", hidden_one, delta_two, preferred_element_type=jnp.float32)
    back_one = jnp.einsum("rk,hk->rh", delta_two, second_weight, preferred_element_type=jnp.float32)
    one_values = hidden_one.astype(jnp.float32)
    delta_one = (back_one * (1.0 - one_values * one_values)).astype(jnp.bfloat16)
    grad_first = jnp.einsum("rf,rh->fh", features, delta_one, preferred_element_type=jnp.float32)
    grad_first, grad_second, grad_output = gradient_sum((grad_first, grad_second, grad_output))
    return (predicted, grad_first, grad_second, grad_output)


def solution(mesh):
    return jax.shard_map(
        on_device,
        mesh=mesh,
        in_specs=(
            P(),
            P("px", "py", None),
            P(None, "px", "py", None),
            P(None, "px", "py", None),
            P(None, None, "px", "py", None),
            P(),
            P(),
            P(),
            P(),
        ),
        out_specs=(P(None, "px", "py", None), P(), P(), P()),
        check_vma=False,
    )
```

```python
import jax
import jax.numpy as jnp
from jax import lax
from jax.sharding import PartitionSpec as P

SLAB = 32
FEAT = 256
TWO_PI = 6.283185307179586
PRECISION = lax.Precision.HIGH


def angles(count_in, count_out, length):
    rows = lax.broadcasted_iota(jnp.int32, (count_in, count_out), 0)
    columns = lax.broadcasted_iota(jnp.int32, (count_in, count_out), 1)
    angle = (rows * columns % length).astype(jnp.float32) * (TWO_PI / length)
    return jnp.cos(angle), jnp.sin(angle)


def complex_table(count_in, count_out, length, sign):
    cosine, sine = angles(count_in, count_out, length)
    top = jnp.stack([cosine, sign * sine], 1)
    bottom = jnp.stack([-sign * sine, cosine], 1)
    return jnp.stack([top, bottom], 0)


def contract(form, values, table):
    return jnp.einsum(form, values, table, precision=PRECISION)


def round_trip(fields, kernel_real, kernel_imag, direction, tables, ranks, x_inverse=None):
    x_forward, y_forward, z_forward, z_inverse, y_inverse, x_full = tables
    if x_inverse is None:
        x_inverse = x_full
    px_size, py_size = ranks
    spectrum = contract("fyzx,xckl->kcfyzl", fields, x_forward)
    spectrum = lax.all_to_all(spectrum, "px", 0, 0, tiled=True)
    spectrum = contract("scfyzl,csydmq->mdzflq", spectrum, y_forward)
    spectrum = lax.all_to_all(spectrum, "py", 0, 0, tiled=True)
    spectrum = contract("sdzflq,dszek->eflqk", spectrum, z_forward)
    real_part = spectrum[0]
    imag_part = spectrum[1]
    product_real = kernel_real * real_part - direction * (kernel_imag * imag_part)
    product_imag = kernel_real * imag_part + direction * (kernel_imag * real_part)
    product = jnp.stack([product_real, product_imag], 0)
    back = contract("eflqk,ekgmz->mgflqz", product, z_inverse)
    back = lax.all_to_all(back, "py", 0, 0, tiled=True)
    back = contract("sgflqz,gsqhmy->mhlfyz", back, y_inverse)
    back = lax.all_to_all(back, "px", 0, 0, tiled=True)
    return contract("shlfyz,hslx->fyzx", back, x_inverse)


def gradient_sum(parts):
    devices = lax.axis_size("px") * lax.axis_size("py")
    joined = jnp.concatenate(parts, 1)
    rows, columns = joined.shape
    share = rows // devices
    summed = lax.all_to_all(joined.reshape(devices, share, columns), ("px", "py"), 0, 0, tiled=True)
    summed = summed.sum(0)
    gathered = jnp.broadcast_to(summed[None], (devices, share, columns))
    gathered = lax.all_to_all(gathered, ("px", "py"), 0, 0, tiled=True).reshape(rows, columns)
    result = []
    offset = 0
    for part in parts:
        result.append(gathered[:, offset : offset + part.shape[1]])
        offset += part.shape[1]
    return tuple(result)


def on_device(
    slab_start,
    fixed_mask,
    background,
    observed,
    kernel,
    frequencies,
    first_weight,
    second_weight,
    output_weight,
):
    y_count, z_count, grid = fixed_mask.shape
    length = kernel.shape[4]
    px_size = lax.axis_size("px")
    py_size = lax.axis_size("py")
    kx_count = kernel.shape[2]
    ky_count = kernel.shape[3]
    first_plane = slab_start[0]
    y_coord = (lax.axis_index("px") * y_count + jnp.arange(y_count, dtype=jnp.int32)).astype(
        jnp.float32
    ) / grid
    z_coord = (lax.axis_index("py") * z_count + jnp.arange(z_count, dtype=jnp.int32)).astype(
        jnp.float32
    ) / grid
    x_coord = (first_plane + jnp.arange(SLAB, dtype=jnp.int32)).astype(jnp.float32) / grid
    phase = (
        x_coord[None, None, :, None] * frequencies[0]
        + y_coord[:, None, None, None] * frequencies[1]
        + z_coord[None, :, None, None] * frequencies[2]
    ) * TWO_PI
    features = (
        jnp.concatenate([jnp.sin(phase), jnp.cos(phase)], -1).astype(jnp.bfloat16).reshape(-1, FEAT)
    )
    hidden_one = jnp.tanh(
        jnp.dot(features, first_weight, preferred_element_type=jnp.float32)
    ).astype(jnp.bfloat16)
    hidden_two = jnp.tanh(
        jnp.dot(hidden_one, second_weight, preferred_element_type=jnp.float32)
    ).astype(jnp.bfloat16)
    network = jnp.einsum("rh,hc->cr", hidden_two, output_weight, preferred_element_type=jnp.float32)
    slab_values = network.reshape(2, y_count, z_count, SLAB)
    zero = jnp.zeros((), jnp.int32)
    placed = lax.dynamic_update_slice(
        jnp.zeros((2, y_count, z_count, grid), jnp.float32),
        slab_values,
        (zero, zero, zero, first_plane),
    )
    plane_index = jnp.arange(grid, dtype=jnp.int32)
    inside = (plane_index >= first_plane) & (plane_index < first_plane + SLAB)
    fields = jnp.where(inside, placed, fixed_mask.astype(jnp.float32) * background)

    cosine, sine = angles(grid, length, length)
    x_forward = jnp.stack([cosine, -sine], 1).reshape(grid, 2, px_size, kx_count)
    y_forward = complex_table(grid, length, length, -1.0).reshape(
        2, px_size, y_count, 2, py_size, ky_count
    )
    z_forward = complex_table(grid, length, length, -1.0).reshape(2, py_size, z_count, 2, length)
    z_inverse = complex_table(length, grid, length, 1.0).reshape(2, length, 2, py_size, z_count)
    y_inverse = complex_table(length, grid, length, 1.0).reshape(
        2, py_size, ky_count, 2, px_size, y_count
    )
    x_inverse = (
        jnp.stack([cosine.T, -sine.T], 0) * (1.0 / float(length) ** 3)
    ).reshape(2, px_size, kx_count, grid)
    tables = (x_forward, y_forward, z_forward, z_inverse, y_inverse, x_inverse)
    ranks = (px_size, py_size)

    kernel_real = kernel[:, 0]
    kernel_imag = kernel[:, 1]
    predicted = round_trip(fields, kernel_real, kernel_imag, 1.0, tables, ranks)
    residual = (predicted - observed) / grid
    slab_inverse = lax.dynamic_slice(x_inverse, (zero, zero, zero, first_plane), (2, px_size, kx_count, SLAB))
    adjoint_slab = round_trip(residual, kernel_real, kernel_imag, -1.0, tables, ranks, slab_inverse)
    cotangent = adjoint_slab.reshape(2, -1).astype(jnp.bfloat16)
    grad_output = jnp.einsum("rh,cr->hc", hidden_two, cotangent, preferred_element_type=jnp.float32)
    back_two = jnp.einsum("cr,hc->rh", cotangent, output_weight, preferred_element_type=jnp.float32)
    two_values = hidden_two.astype(jnp.float32)
    delta_two = (back_two * (1.0 - two_values * two_values)).astype(jnp.bfloat16)
    grad_second = jnp.einsum("rh,rk->hk", hidden_one, delta_two, preferred_element_type=jnp.float32)
    back_one = jnp.einsum("rk,hk->rh", delta_two, second_weight, preferred_element_type=jnp.float32)
    one_values = hidden_one.astype(jnp.float32)
    delta_one = (back_one * (1.0 - one_values * one_values)).astype(jnp.bfloat16)
    grad_first = jnp.einsum("rf,rh->fh", features, delta_one, preferred_element_type=jnp.float32)
    grad_first, grad_second, grad_output = gradient_sum((grad_first, grad_second, grad_output))
    return (predicted, grad_first, grad_second, grad_output)


def solution(mesh):
    return jax.shard_map(
        on_device,
        mesh=mesh,
        in_specs=(
            P(),
            P("px", "py", None),
            P(None, "px", "py", None),
            P(None, "px", "py", None),
            P(None, None, "px", "py", None),
            P(),
            P(),
            P(),
            P(),
        ),
        out_specs=(P(None, "px", "py", None), P(), P(), P()),
        check_vma=False,
    )
```

```python
import jax
import jax.numpy as jnp
from jax import lax
from jax.sharding import PartitionSpec as P

SLAB = 32
FEAT = 256
TWO_PI = 6.283185307179586
PRECISION = lax.Precision.HIGH


def angles(count_in, count_out, length):
    rows = lax.broadcasted_iota(jnp.int32, (count_in, count_out), 0)
    columns = lax.broadcasted_iota(jnp.int32, (count_in, count_out), 1)
    angle = (rows * columns % length).astype(jnp.float32) * (TWO_PI / length)
    return jnp.cos(angle), jnp.sin(angle)


def complex_table(count_in, count_out, length, sign):
    cosine, sine = angles(count_in, count_out, length)
    top = jnp.stack([cosine, sign * sine], 1)
    bottom = jnp.stack([-sign * sine, cosine], 1)
    return jnp.stack([top, bottom], 0)


def contract(form, values, table):
    return jnp.einsum(form, values, table, precision=PRECISION)


def round_trip(fields, kernel_real, kernel_imag, direction, tables, ranks, x_inverse=None):
    x_forward, y_forward, z_forward, z_inverse, y_inverse, x_full = tables
    if x_inverse is None:
        x_inverse = x_full
    px_size, py_size = ranks
    spectrum = contract("fyzx,xckl->kcyfzl", fields, x_forward)
    spectrum = lax.all_to_all(spectrum, "px", 0, 0, tiled=True)
    spectrum = contract("scyfzl,csydmq->mdzflq", spectrum, y_forward)
    spectrum = lax.all_to_all(spectrum, "py", 0, 0, tiled=True)
    spectrum = contract("sdzflq,dszek->eflqk", spectrum, z_forward)
    real_part = spectrum[0]
    imag_part = spectrum[1]
    product_real = kernel_real * real_part - direction * (kernel_imag * imag_part)
    product_imag = kernel_real * imag_part + direction * (kernel_imag * real_part)
    product = jnp.stack([product_real, product_imag], 0)
    back = contract("eflqk,ekgmz->mgflqz", product, z_inverse)
    back = lax.all_to_all(back, "py", 0, 0, tiled=True)
    back = contract("sgflqz,gsqhmy->mhlfyz", back, y_inverse)
    back = lax.all_to_all(back, "px", 0, 0, tiled=True)
    return contract("shlfyz,hslx->fyzx", back, x_inverse)


def gradient_sum(parts):
    devices = lax.axis_size("px") * lax.axis_size("py")
    joined = jnp.concatenate(parts, 1)
    rows, columns = joined.shape
    share = rows // devices
    summed = lax.all_to_all(joined.reshape(devices, share, columns), ("px", "py"), 0, 0, tiled=True)
    summed = summed.sum(0)
    gathered = jnp.broadcast_to(summed[None], (devices, share, columns))
    gathered = lax.all_to_all(gathered, ("px", "py"), 0, 0, tiled=True).reshape(rows, columns)
    result = []
    offset = 0
    for part in parts:
        result.append(gathered[:, offset : offset + part.shape[1]])
        offset += part.shape[1]
    return tuple(result)


def on_device(
    slab_start,
    fixed_mask,
    background,
    observed,
    kernel,
    frequencies,
    first_weight,
    second_weight,
    output_weight,
):
    y_count, z_count, grid = fixed_mask.shape
    length = kernel.shape[4]
    px_size = lax.axis_size("px")
    py_size = lax.axis_size("py")
    kx_count = kernel.shape[2]
    ky_count = kernel.shape[3]
    first_plane = slab_start[0]
    y_coord = (lax.axis_index("px") * y_count + jnp.arange(y_count, dtype=jnp.int32)).astype(
        jnp.float32
    ) / grid
    z_coord = (lax.axis_index("py") * z_count + jnp.arange(z_count, dtype=jnp.int32)).astype(
        jnp.float32
    ) / grid
    x_coord = (first_plane + jnp.arange(SLAB, dtype=jnp.int32)).astype(jnp.float32) / grid
    phase = (
        x_coord[None, None, :, None] * frequencies[0]
        + y_coord[:, None, None, None] * frequencies[1]
        + z_coord[None, :, None, None] * frequencies[2]
    ) * TWO_PI
    features = (
        jnp.concatenate([jnp.sin(phase), jnp.cos(phase)], -1).astype(jnp.bfloat16).reshape(-1, FEAT)
    )
    hidden_one = jnp.tanh(
        jnp.dot(features, first_weight, preferred_element_type=jnp.float32)
    ).astype(jnp.bfloat16)
    hidden_two = jnp.tanh(
        jnp.dot(hidden_one, second_weight, preferred_element_type=jnp.float32)
    ).astype(jnp.bfloat16)
    network = jnp.einsum("rh,hc->cr", hidden_two, output_weight, preferred_element_type=jnp.float32)
    slab_values = network.reshape(2, y_count, z_count, SLAB)
    zero = jnp.zeros((), jnp.int32)
    placed = lax.dynamic_update_slice(
        jnp.zeros((2, y_count, z_count, grid), jnp.float32),
        slab_values,
        (zero, zero, zero, first_plane),
    )
    plane_index = jnp.arange(grid, dtype=jnp.int32)
    inside = (plane_index >= first_plane) & (plane_index < first_plane + SLAB)
    fields = jnp.where(inside, placed, fixed_mask.astype(jnp.float32) * background)

    cosine, sine = angles(grid, length, length)
    x_forward = jnp.stack([cosine, -sine], 1).reshape(grid, 2, px_size, kx_count)
    y_forward = complex_table(grid, length, length, -1.0).reshape(
        2, px_size, y_count, 2, py_size, ky_count
    )
    z_forward = complex_table(grid, length, length, -1.0).reshape(2, py_size, z_count, 2, length)
    z_inverse = complex_table(length, grid, length, 1.0).reshape(2, length, 2, py_size, z_count)
    y_inverse = complex_table(length, grid, length, 1.0).reshape(
        2, py_size, ky_count, 2, px_size, y_count
    )
    x_inverse = (
        jnp.stack([cosine.T, -sine.T], 0) * (1.0 / float(length) ** 3)
    ).reshape(2, px_size, kx_count, grid)
    tables = (x_forward, y_forward, z_forward, z_inverse, y_inverse, x_inverse)
    ranks = (px_size, py_size)

    kernel_real = kernel[:, 0]
    kernel_imag = kernel[:, 1]
    predicted = round_trip(fields, kernel_real, kernel_imag, 1.0, tables, ranks)
    residual = (predicted - observed) / grid
    slab_inverse = lax.dynamic_slice(x_inverse, (zero, zero, zero, first_plane), (2, px_size, kx_count, SLAB))
    adjoint_slab = round_trip(residual, kernel_real, kernel_imag, -1.0, tables, ranks, slab_inverse)
    cotangent = adjoint_slab.reshape(2, -1).astype(jnp.bfloat16)
    grad_output = jnp.einsum("rh,cr->hc", hidden_two, cotangent, preferred_element_type=jnp.float32)
    back_two = jnp.einsum("cr,hc->rh", cotangent, output_weight, preferred_element_type=jnp.float32)
    two_values = hidden_two.astype(jnp.float32)
    delta_two = (back_two * (1.0 - two_values * two_values)).astype(jnp.bfloat16)
    grad_second = jnp.einsum("rh,rk->hk", hidden_one, delta_two, preferred_element_type=jnp.float32)
    back_one = jnp.einsum("rk,hk->rh", delta_two, second_weight, preferred_element_type=jnp.float32)
    one_values = hidden_one.astype(jnp.float32)
    delta_one = (back_one * (1.0 - one_values * one_values)).astype(jnp.bfloat16)
    grad_first = jnp.einsum("rf,rh->fh", features, delta_one, preferred_element_type=jnp.float32)
    grad_first, grad_second, grad_output = gradient_sum((grad_first, grad_second, grad_output))
    return (predicted, grad_first, grad_second, grad_output)


def solution(mesh):
    return jax.shard_map(
        on_device,
        mesh=mesh,
        in_specs=(
            P(),
            P("px", "py", None),
            P(None, "px", "py", None),
            P(None, "px", "py", None),
            P(None, None, "px", "py", None),
            P(),
            P(),
            P(),
            P(),
        ),
        out_specs=(P(None, "px", "py", None), P(), P(), P()),
        check_vma=False,
    )
```
